32 devices in a mesh: shot: 2 (over core), probe: 16 (over z, y, x).
Axes of the slice: x: 2, y: 2, z: 4, core: 2. Of those that a mesh axis runs over, the one named last changes fastest.
Arguments:
- probes: float32 [32, 256, 512], P('probe'), may hold values from -6 to 6
- coarse_sample: float32 [32, 256, 512], P('probe', 'shot'), may hold values from -6 to 6
- coefficient: float32 [256, 512], replicated, may hold values from 0.05 to 0.45
- receiver: float32 [256, 512], replicated, may hold values from 0.05 to 0.5
- checkpoints: float32 [4, 2, 256, 512], P('shot', None, 'probe'), may hold values from -6 to 6
- encodings: int32 [4, 256], P('shot'), may hold values from -1 to 1, as said below
- wavelet: float32 [3, 256], replicated, may hold values from -6 to 6
- bounds: int32 [33], replicated, may hold values from 0 to 256, as said below
Outputs:
- samples: float32 [32, 256, 512], P('probe', 'shot')
The draws below stay inside these ranges and needn't reach their ends.
Inputs may be any that keep to these rules, and one draw needn't show every extreme that they name: `encodings`: every entry is -1 or 1. bounds[0] = 0 and bounds[32] = 256; the entries rise strictly; blocks 2 i and 2 i + 1 together hold exactly 16 rows.
All inputs are finite; a program needn't handle non-finite values.
Results may differ from the reference program's by a relative error of at most 0.000094.
Values sent between devices are 32-bit elements; how exact they have to be, the bound alone decides.
A program may use at most 128 MiB of HBM per device.

```python
import math
import jax
import jax.numpy as jnp
from jax import lax

NZ = 512
NSHOT = 256
NT = 4
BLK = 8
NX = 256
SUPER = 4
PROBES = 32
NB = 32


def draw_encodings(key, part):
    signs = jax.random.randint(key, (SUPER, NSHOT), 0, 2)
    return (signs * 2 - 1).astype(jnp.int32)


def draw_bounds(key, part):
    half = BLK // 2
    offset = jax.random.randint(key, (NB // 2,), 1 - half, half)
    sizes = jnp.stack([BLK + offset, BLK - offset], axis=1).reshape(-1)
    return jnp.concatenate([jnp.zeros((1,), jnp.int32), jnp.cumsum(sizes).astype(jnp.int32)])


def block_scale(rng, extent, pieces, smallest, high):
    def one(dim, parts):
        steps = jax.random.uniform(jax.random.fold_in(jax.random.fold_in(rng, 6), dim), (parts,), jnp.float32, smallest / len(pieces), high / len(pieces))
        return jnp.repeat(jnp.exp(steps), extent[dim] // parts).reshape((-1,) + (1,) * (len(extent) - dim - 1))

    factor_of = one(*pieces[0])
    for cut in pieces[1:]:
        factor_of = factor_of * one(*cut)
    return factor_of


def gaussian(key, dims, spread, limit, shards=(), held_as=jnp.bfloat16):
    result = spread * jax.random.normal(key, dims, jnp.float32)
    if shards:
        result = result * block_scale(key, dims, shards, -0.22, 0.18)
    return jnp.clip(result, -limit, limit).astype(held_as)


def setup_inputs(seed: int = 0) -> dict:
    streams_of = jax.random.split(jax.random.key(seed), 9)
    return {
        "probes": gaussian(streams_of[0], (PROBES, NX, NZ), 1.0, 6.0, ((0, 16),), jnp.float32),
        "coarse_sample": gaussian(streams_of[1], (PROBES, NX, NZ), 1.0, 6.0, ((0, 16), (1, 2)), jnp.float32),
        "coefficient": jnp.clip(jnp.exp(jax.random.uniform(streams_of[2], (NX, NZ), jnp.float32, math.log(0.05), math.log(0.45))), 0.05, 0.45),
        "receiver": jnp.clip(jnp.exp(jax.random.uniform(streams_of[3], (NX, NZ), jnp.float32, math.log(0.05), math.log(0.5))), 0.05, 0.5),
        "checkpoints": gaussian(streams_of[4], (SUPER, 2, NX, NZ), 1.0, 6.0, ((0, 2), (2, 16)), jnp.float32),
        "encodings": draw_encodings(jax.random.fold_in(streams_of[8], 71), 0),
        "wavelet": gaussian(streams_of[6], (NT - 1, NSHOT), 1.0, 6.0, (), jnp.float32),
        "bounds": draw_bounds(jax.random.fold_in(streams_of[8], 71), 0),
    }


def laplace(values):
    pad_width = [(0, 0)] * (values.ndim - 2) + [(1, 1), (1, 1)]
    padded = jnp.pad(values, pad_width)
    return padded[..., 2:, 1:-1] + padded[..., :-2, 1:-1] + padded[..., 1:-1, 2:] + padded[..., 1:-1, :-2] - 4.0 * values

def shot_sources(encodings, wavelet):
    columns = jnp.arange(NZ)
    spacing = NZ // NSHOT
    position = jnp.arange(NSHOT) * NZ // NSHOT + spacing // 2
    onehot = (position[:, None] == columns[None, :]).astype(jnp.float32)
    amplitude = encodings.astype(jnp.float32)[:, None, :] * wavelet[None, :, :]
    return jnp.einsum('stk,kz->stz', amplitude, onehot, precision=lax.Precision.HIGHEST)

def block_parity(row_index, bounds):
    inner = bounds[1:-1]
    return lax.optimization_barrier(jnp.sum((row_index[:, None] >= inner[None, :]).astype(jnp.int32), axis=1)) % 2

def forward_levels(pair, source_rows, coefficient):
    at_source = (jnp.arange(NX) == NX // 2).astype(jnp.float32)[:, None]
    before = pair[0]
    current = pair[1]
    history = [current]
    for moment in range(NT - 1):
        following = 2.0 * current - before + coefficient * laplace(current) + at_source * source_rows[moment][None, :]
        before, current = (current, following)
        history.append(current)
    return jnp.stack(history)

def increments(vectors, levels, coefficient, receiver):
    before = jnp.zeros_like(vectors)
    current = jnp.zeros_like(vectors)
    observed = []
    for moment in range(NT):
        following = 2.0 * current - before + coefficient * laplace(current) + vectors * levels[moment]
        before, current = (current, following)
        observed.append(receiver * following)
    return jnp.stack(observed)

def reference(probes, coarse_sample, coefficient, receiver, checkpoints, encodings, wavelet, bounds):
    parity = block_parity(jnp.arange(NX), bounds)
    colour = jnp.arange(PROBES) % 2
    support = (parity[None, :] == colour[:, None]).astype(jnp.float32)
    vectors = probes * support[:, :, None]
    sources = shot_sources(encodings, wavelet)

    def one_shot(accumulated, inputs):
        pair, source_rows = inputs
        levels = forward_levels(pair, source_rows, coefficient)

        def observe(moved):
            return increments(moved, levels, coefficient, receiver)
        observed, pullback = jax.vjp(observe, vectors)
        gradient, = pullback(observed)
        return (accumulated + gradient, None)
    hessian, _ = lax.scan(one_shot, jnp.zeros_like(vectors), (checkpoints, sources))
    keep = (parity[None, :] != colour[:, None]).astype(jnp.float32)
    return keep[:, :, None] * (hessian - coarse_sample)
```

```python
import functools

import jax
import jax.numpy as jnp
from jax import lax
from jax.experimental import pallas as pl
from jax.experimental.pallas import tpu as pltpu
from jax.sharding import PartitionSpec as P

MESH = pl.DeviceIdType.MESH
SUB = 8
LANE = 128
INNER = 4


def kernel(
    num_shot_devices,
    num_probe_devices,
    bounds_ref,
    encodings_ref,
    wavelet_ref,
    probes_hbm,
    coarse_hbm,
    coefficient_hbm,
    receiver_hbm,
    checkpoints_hbm,
    out_ref,
    gathered,
    probes_in,
    coarse_in,
    coefficient_in,
    receiver_in,
    coef,
    centre,
    weight,
    vec,
    um,
    u0,
    u1,
    u2,
    u3,
    d1,
    d2,
    d3,
    e4,
    e3,
    e2,
    total,
    flat,
    partial,
    inverse,
    parity_out,
    source,
    load_sem,
    own_sem,
    recv_sem,
    send_sem,
    swap_send,
    swap_recv,
):
    members, _, chunk, width = checkpoints_hbm.shape
    num_probes, num_rows, _ = probes_hbm.shape
    out_rows = coarse_hbm.shape[1]
    tiles = num_rows // SUB
    cols = [pl.ds(c * LANE, LANE) for c in range(width // LANE)]
    steps = wavelet_ref.shape[0]
    line = num_probe_devices // INNER
    flags = num_probe_devices * 2

    shot = lax.axis_index("shot")
    mine = lax.axis_index("probe")
    z = mine // INNER
    a = mine % INNER
    high, low = a // 2, a % 2
    right = 2 * low + (1 - high)
    left = 2 * (1 - low) + high

    places = {"a": a, "right": right, "left": left, "far": 3 - a}
    ids = {
        (dz, name): (z + dz) * INNER + place
        for dz in range(1 - line, line)
        for name, place in places.items()
    }
    toward = {1: z < line - 1, -1: z > 0}
    exists = {dz: (z + dz >= 0) & (z + dz < line) for dz in range(1 - line, line)}
    passes = {
        (dz, sign): exists[dz] & toward[sign] for dz in range(1 - line, line) for sign in (1, -1)
    }

    def slot(m, src, t):
        first = pl.multiple_of((src * 2 + t) * chunk, chunk)
        return gathered.at[m, :, pl.ds(first, chunk), :]

    def own_copy(m, t):
        first = pl.multiple_of((mine * 2 + t) * chunk, chunk)
        return [
            pltpu.make_async_copy(
                checkpoints_hbm.at[m, t, :, c],
                gathered.at[m, i, pl.ds(first, chunk), :],
                own_sem.at[(m * 2 + t) * len(cols) + i],
            )
            for i, c in enumerate(cols)
        ]

    for m in range(members):
        for t in range(2):
            for copy in own_copy(m, t):
                copy.start()

    count = len(cols)
    load_probes = [
        pltpu.make_async_copy(probes_hbm.at[:, :, c], probes_in.at[:, i], load_sem.at[i])
        for i, c in enumerate(cols)
    ]
    load_coefficient = [
        pltpu.make_async_copy(coefficient_hbm.at[:, c], coefficient_in.at[i], load_sem.at[count + i])
        for i, c in enumerate(cols)
    ]
    load_receiver = [
        pltpu.make_async_copy(receiver_hbm.at[:, c], receiver_in.at[i], load_sem.at[2 * count + i])
        for i, c in enumerate(cols)
    ]
    load_coarse = [pltpu.make_async_copy(coarse_hbm, coarse_in, load_sem.at[3 * count])]
    for load in load_coefficient + load_receiver + load_probes + load_coarse:
        load.start()

    barrier = pltpu.get_barrier_semaphore()

    def greet(device):
        pl.semaphore_signal(barrier, inc=1, device_id=device, device_id_type=MESH)

    greet({"probe": ids[0, "right"]})
    greet({"probe": ids[0, "left"]})

    @pl.when(z > 0)
    def _():
        greet({"probe": ids[-1, "a"]})

    @pl.when(z < line - 1)
    def _():
        greet({"probe": ids[1, "a"]})

    for away in range(1, num_shot_devices):
        greet({"shot": (shot + away) % num_shot_devices})
    inside = jnp.where(z > 0, 1, 0) + jnp.where(z < line - 1, 1, 0)
    pl.semaphore_wait(barrier, inside + 2 + num_shot_devices - 1)

    sent = []

    def send(m, src, t, target, lane, cond=None):
        def copy():
            return pltpu.make_async_remote_copy(
                src_ref=slot(m, ids[src], t),
                dst_ref=slot(m, ids[src], t),
                send_sem=send_sem.at[(lane * members + m) * flags + ids[src] * 2 + t],
                recv_sem=recv_sem.at[m * flags + ids[src] * 2 + t],
                device_id={"probe": ids[target]},
                device_id_type=MESH,
            )

        copy().start()
        sent.append((copy, cond))

    def arrive(m, src, t):
        pltpu.make_async_remote_copy(
            src_ref=slot(m, ids[src], t),
            dst_ref=slot(m, ids[src], t),
            send_sem=send_sem.at[m * flags + ids[src] * 2 + t],
            recv_sem=recv_sem.at[m * flags + ids[src] * 2 + t],
            device_id={"probe": ids[0, "right"]},
            device_id_type=MESH,
        ).wait_recv()

    def spread(m, src, cond=None):
        for t in (0, 1):
            send(m, src, t, (0, "right"), 2, cond)
            send(m, src, 1 - t, (0, "left"), 3, cond)

    def column(m, k):
        if k == 0:
            for t in range(2):
                for copy in own_copy(m, t):
                    copy.wait()
            for sign, lane in ((1, 0), (-1, 1)):

                @pl.when(toward[sign])
                def _(sign=sign, lane=lane):
                    for t in (0, 1):
                        send(m, (0, "a"), t, (sign, "a"), lane, toward[sign])

            spread(m, (0, "a"))
            return
        for sign, lane in ((1, 0), (-1, 1)):
            src = (-sign * k, "a")
            here = exists[-sign * k]
            more = passes[-sign * k, sign]

            @pl.when(here)
            def _(src=src):
                for t in (0, 1):
                    arrive(m, src, t)

            @pl.when(more)
            def _(src=src, sign=sign, lane=lane, more=more):
                for t in (0, 1):
                    send(m, src, t, (sign, "a"), lane, more)

            @pl.when(here)
            def _(src=src, here=here):
                spread(m, src, here)

    def sides(k):
        if k == 0:
            return ((0, None),)
        return ((-k, exists[-k]), (k, exists[k]))

    def guarded(cond, fun):
        if cond is None:
            fun()
        else:
            pl.when(cond)(fun)

    def relay(m, k):
        for dz, cond in sides(k):

            def run(dz=dz, cond=cond):
                arrive(m, (dz, "left"), 0)
                send(m, (dz, "left"), 0, (0, "right"), 2, cond)
                arrive(m, (dz, "right"), 1)
                send(m, (dz, "right"), 1, (0, "left"), 3, cond)

            guarded(cond, run)

    def finish(m, k):
        for dz, cond in sides(k):

            def run(dz=dz):
                arrive(m, (dz, "left"), 1)
                arrive(m, (dz, "right"), 0)
                arrive(m, (dz, "far"), 0)
                arrive(m, (dz, "far"), 1)

            guarded(cond, run)

    def gather_steps(m):
        plan = [lambda: column(m, 0)]
        for k in range(1, line):
            plan.append(lambda k=k: column(m, k))
            plan.append(lambda k=k: relay(m, k - 1))
        plan.append(lambda: relay(m, line - 1))
        return plan

    def gather_end(m):
        for k in range(line):
            finish(m, k)

    first_plan = gather_steps(0)
    first_plan[0]()

    row_in_tile = lax.broadcasted_iota(jnp.int32, (SUB, LANE), 0)
    lane_index = lax.broadcasted_iota(jnp.int32, (SUB, LANE), 1)
    at_first = lane_index == 0
    at_last = lane_index == LANE - 1

    def parity_of(rows):
        count = jnp.zeros((SUB, LANE), jnp.int32)
        for b in range(1, bounds_ref.shape[0] - 1):
            count = count + jnp.where(rows >= bounds_ref[b], 1, 0)
        return count % 2

    def prepare_sources():
        shots = wavelet_ref.shape[1]
        spacing = width // shots
        k = lax.broadcasted_iota(jnp.int32, (shots, width), 0)
        position = k * width // shots + spacing // 2
        column_index = lax.broadcasted_iota(jnp.int32, (shots, width), 1)
        onehot = jnp.where(position == column_index, 1.0, 0.0)
        for m in range(members):
            amplitude = encodings_ref[m : m + 1, :].astype(jnp.float32) * wavelet_ref[...]
            source[m, 0:steps, :] = jnp.dot(
                amplitude,
                onehot,
                precision=lax.Precision.HIGHEST,
                preferred_element_type=jnp.float32,
            )

    def strided(j):
        return pl.ds(j, SUB, stride=tiles)

    def prepare_fields():
        def body(j, carry):
            parity = parity_of(row_in_tile * tiles + j)
            for i, c in enumerate(cols):
                value = coefficient_in[i, strided(j), :]
                seen = receiver_in[i, strided(j), :]
                coef[j, :, c] = value
                centre[j, :, c] = 2.0 - 4.0 * value
                weight[j, :, c] = value * (seen * seen)
                for p in range(num_probes):
                    vec[p, j, :, c] = jnp.where(
                        parity == p % 2, probes_in[p, i, strided(j), :], 0.0
                    )
            return carry

        lax.fori_loop(0, tiles, body, 0)

    def prepare_out():
        def body(i, carry):
            first = shot * out_rows + i * SUB
            parity_out[i] = parity_of(row_in_tile + first)
            for n, c in enumerate(cols):
                rows = pl.ds(pl.multiple_of(first, SUB), SUB)
                inverse[i, :, c] = 1.0 / coefficient_in[n, rows, :]
            return carry

        lax.fori_loop(0, out_rows // SUB, body, 0)

    def halo(field):
        for c in cols:
            above = pltpu.roll(field[tiles, :, c], 1, 0)
            field[0, :, c] = jnp.where(row_in_tile == 0, 0.0, above)
            below = pltpu.roll(field[1, :, c], SUB - 1, 0)
            field[tiles + 1, :, c] = jnp.where(row_in_tile == SUB - 1, 0.0, below)

    def around(field, j):
        here = [field[j + 1, :, c] for c in cols]
        fore = [pltpu.roll(x, 1, 1) for x in here]
        back = [pltpu.roll(x, LANE - 1, 1) for x in here]
        near = []
        for i, c in enumerate(cols):
            west = jnp.where(at_first, fore[i - 1] if i else 0.0, fore[i])
            east = jnp.where(at_last, back[i + 1] if i + 1 < len(cols) else 0.0, back[i])
            near.append((field[j, :, c] + field[j + 2, :, c]) + (west + east))
        return here, near

    def advance(field, before, j):
        here, near = around(field, j)
        moved = []
        for i, c in enumerate(cols):
            value = centre[j, :, c] * here[i] + coef[j, :, c] * near[i]
            if before is not None:
                value = value - before(j, c)
            moved.append(value)
        return moved

    def inner(field):
        return lambda j, c: field[j + 1, :, c]

    def convert(m):
        per = tiles // chunk
        for block in range(per):

            def body(r, carry, block=block):
                j = block * chunk + r
                for i, c in enumerate(cols):
                    um[j, :, c] = gathered[
                        m, i, pl.ds((block * 2) * chunk + r, SUB, stride=2 * tiles), :
                    ]
                    value = gathered[
                        m, i, pl.ds((block * 2 + 1) * chunk + r, SUB, stride=2 * tiles), :
                    ]
                    u0[j + 1, :, c] = value
                    for p in range(num_probes):
                        d1[p, j + 1, :, c] = vec[p, j, :, c] * value
                return carry

            lax.fori_loop(0, chunk, body, 0)
        halo(u0)
        for p in range(num_probes):
            halo(d1.at[p])

    def forward(m, t):
        field = (u0, u1, u2)[t]
        before = (lambda j, c: um[j, :, c], inner(u0), inner(u1))[t]
        result = (u1, u2, u3)[t]
        delta = (d1, d2, d3)[t]
        delta_before = (None, d1, d2)[t]
        delta_next = (d2, d3, e4)[t]

        def body(j, first):
            moved = advance(field, before, j)
            if first:
                for i, c in enumerate(cols):
                    row = jnp.broadcast_to(source[m, t : t + 1, c], (SUB, LANE))
                    moved[i] = moved[i] + jnp.where(row_in_tile == SUB // 2, row, 0.0)
            for i, c in enumerate(cols):
                result[j + 1, :, c] = moved[i]
            for p in range(num_probes):
                prior = None if delta_before is None else inner(delta_before.at[p])
                step = advance(delta.at[p], prior, j)
                for i, c in enumerate(cols):
                    value = step[i] + vec[p, j, :, c] * moved[i]
                    if t < 2:
                        delta_next[p, j + 1, :, c] = value
                    else:
                        value = weight[j, :, c] * value
                        delta_next[p, j + 1, :, c] = value
                        gain = moved[i] * value
                        if m:
                            gain = total[p, j, :, c] + gain
                        total[p, j, :, c] = gain

        body(0, True)

        def rest(j, carry):
            body(j, False)
            return carry

        lax.fori_loop(1, tiles, rest, 0)
        if t < 2:
            halo(result)
        for p in range(num_probes):
            halo(delta_next.at[p])

    def adjoint(m, t, which):
        field = (e4, e3, e2)[t]
        before = (None, e4, e3)[t]
        result = (e3, e2, None)[t]
        delta = (d3, d2, d1)[t]
        level = (u2, u1, u0)[t]

        def body(j, carry):
            for p in which:
                prior = None if before is None else inner(before.at[p])
                step = advance(field.at[p], prior, j)
                for i, c in enumerate(cols):
                    value = step[i] + weight[j, :, c] * delta[p, j + 1, :, c]
                    if result is not None:
                        result[p, j + 1, :, c] = value
                    gain = total[p, j, :, c] + level[j + 1, :, c] * value
                    if result is None and m == members - 1:
                        flat[p, i, strided(j), :] = gain
                    else:
                        total[p, j, :, c] = gain
            return carry

        lax.fori_loop(0, tiles, body, 0)
        if result is not None:
            for p in which:
                halo(result.at[p])

    def swap(p):
        copies = []
        for away in range(1, num_shot_devices):
            other = (shot + away) % num_shot_devices
            copies.append(
                pltpu.make_async_remote_copy(
                    src_ref=flat.at[p, :, pl.ds(pl.multiple_of(other * out_rows, SUB), out_rows), :],
                    dst_ref=partial.at[away - 1, p],
                    send_sem=swap_send.at[away - 1, p],
                    recv_sem=swap_recv.at[away - 1, p],
                    device_id={"shot": other},
                    device_id_type=MESH,
                )
            )
        return copies

    def combine(p):
        def body(i, carry):
            first = pl.multiple_of(shot * out_rows + i * SUB, SUB)
            local = pl.ds(pl.multiple_of(i * SUB, SUB), SUB)
            keep = parity_out[i] != p % 2
            for n, c in enumerate(cols):
                value = flat[p, n, pl.ds(first, SUB), :]
                for away in range(1, num_shot_devices):
                    value = value + partial[away - 1, p, n, local, :]
                value = value * inverse[i, :, c] - coarse_in[p, local, c]
                out_ref[p, local, c] = jnp.where(keep, value, 0.0)
            return carry

        lax.fori_loop(0, out_rows // SUB, body, 0)

    everything = tuple(range(num_probes))
    prepare_sources()
    for load in load_coefficient:
        load.wait()
    first_plan[1]()
    first_plan[2]()
    prepare_out()
    first_plan[3]()
    for load in load_probes + load_receiver:
        load.wait()
    prepare_fields()
    for step in first_plan[4:]:
        step()
    load_coarse[0].wait()
    copies = [None] * num_probes
    for m in range(members):
        plan = gather_steps(m + 1) if m + 1 < members else []
        if plan:
            plan.pop(0)()
        gather_end(m)
        stages = [lambda: convert(m)]
        stages += [lambda t=t: forward(m, t) for t in range(3)]
        stages += [lambda t=t: adjoint(m, t, everything) for t in range(2)]
        if m < members - 1:
            stages.append(lambda: adjoint(m, 2, everything))
        for stage in stages:
            stage()
            if plan:
                plan.pop(0)()
        for step in plan:
            step()
    for p in everything:
        adjoint(members - 1, 2, (p,))
        copies[p] = swap(p)
        for copy in copies[p]:
            copy.start()
    for p in everything:
        for copy in copies[p]:
            copy.wait_recv()
        combine(p)
    for p in everything:
        for copy in copies[p]:
            copy.wait_send()
    for copy, cond in sent:
        guarded(cond, lambda copy=copy: copy().wait_send())


def on_device(
    num_shot_devices,
    num_probe_devices,
    probes,
    coarse_sample,
    coefficient,
    receiver,
    checkpoints,
    encodings,
    wavelet,
    bounds,
):
    members, levels, chunk, width = checkpoints.shape
    num_probes, num_rows, _ = probes.shape
    out_rows = coarse_sample.shape[1]
    tiles = num_rows // SUB
    groups = width // LANE
    f32 = jnp.float32

    def plain(*lead):
        return pltpu.VMEM((*lead, tiles, SUB, width), f32)

    def ringed(*lead):
        return pltpu.VMEM((*lead, tiles + 2, SUB, width), f32)

    others = num_shot_devices - 1
    anywhere = pl.BlockSpec(memory_space=pl.ANY)
    vmem = pl.BlockSpec(memory_space=pltpu.VMEM)
    return pl.pallas_call(
        functools.partial(kernel, num_shot_devices, num_probe_devices),
        out_shape=jax.ShapeDtypeStruct(coarse_sample.shape, f32),
        in_specs=[pl.BlockSpec(memory_space=pltpu.SMEM), vmem, vmem] + [anywhere] * 5,
        out_specs=vmem,
        scratch_shapes=[
            pltpu.VMEM((members, groups, levels * num_rows, LANE), f32),
            pltpu.VMEM((num_probes, groups, num_rows, LANE), f32),
            pltpu.VMEM(coarse_sample.shape, f32),
            pltpu.VMEM((groups, num_rows, LANE), f32),
            pltpu.VMEM((groups, num_rows, LANE), f32),
            plain(),
            plain(),
            plain(),
            plain(num_probes),
            plain(),
            ringed(),
            ringed(),
            ringed(),
            ringed(),
            ringed(num_probes),
            ringed(num_probes),
            ringed(num_probes),
            ringed(num_probes),
            ringed(num_probes),
            ringed(num_probes),
            plain(num_probes),
            pltpu.VMEM((num_probes, groups, num_rows, LANE), f32),
            pltpu.VMEM((others, num_probes, groups, out_rows, LANE), f32),
            pltpu.VMEM((out_rows // SUB, SUB, width), f32),
            pltpu.VMEM((out_rows // SUB, SUB, LANE), jnp.int32),
            pltpu.VMEM((members, SUB, width), f32),
            pltpu.SemaphoreType.DMA((3 * groups + 1,)),
            pltpu.SemaphoreType.DMA((members * levels * groups,)),
            pltpu.SemaphoreType.DMA((members * num_probe_devices * levels,)),
            pltpu.SemaphoreType.DMA((4 * members * num_probe_devices * levels,)),
            pltpu.SemaphoreType.DMA((others, num_probes)),
            pltpu.SemaphoreType.DMA((others, num_probes)),
        ],
        compiler_params=pltpu.CompilerParams(
            collective_id=0, has_side_effects=True, vmem_limit_bytes=60 * 1024 * 1024
        ),
    )(
        bounds,
        encodings,
        wavelet,
        probes,
        coarse_sample,
        coefficient,
        receiver,
        checkpoints,
    )


def solution(mesh):
    return jax.shard_map(
        functools.partial(on_device, mesh.shape["shot"], mesh.shape["probe"]),
        mesh=mesh,
        in_specs=(
            P("probe", None, None),
            P("probe", "shot", None),
            P(),
            P(),
            P("shot", None, "probe", None),
            P("shot", None),
            P(),
            P(),
        ),
        out_specs=P("probe", "shot", None),
        check_vma=False,
    )
```

```python
import functools

import jax
import jax.numpy as jnp
from jax import lax
from jax.experimental import pallas as pl
from jax.experimental.pallas import tpu as pltpu
from jax.sharding import PartitionSpec as P

MESH = pl.DeviceIdType.MESH
SUB = 8
LANE = 128
INNER = 4


def kernel(
    num_shot_devices,
    num_probe_devices,
    bounds_ref,
    encodings_ref,
    wavelet_ref,
    probes_hbm,
    coarse_hbm,
    coefficient_hbm,
    receiver_hbm,
    checkpoints_hbm,
    out_ref,
    gathered,
    probes_in,
    coarse_in,
    coefficient_in,
    receiver_in,
    coef,
    centre,
    weight,
    vec,
    um,
    u0,
    u1,
    u2,
    u3,
    d1,
    d2,
    d3,
    e4,
    e3,
    e2,
    total,
    flat,
    partial,
    inverse,
    parity_out,
    source,
    load_sem,
    own_sem,
    recv_sem,
    send_sem,
    line_sem,
    swap_send,
    swap_recv,
):
    members, _, chunk, width = checkpoints_hbm.shape
    num_probes, num_rows, _ = probes_hbm.shape
    out_rows = coarse_hbm.shape[1]
    tiles = num_rows // SUB
    cols = [pl.ds(c * LANE, LANE) for c in range(width // LANE)]
    steps = wavelet_ref.shape[0]
    line = num_probe_devices // INNER
    flags = num_probe_devices * 2

    shot = lax.axis_index("shot")
    mine = lax.axis_index("probe")
    z = mine // INNER
    a = mine % INNER
    high, low = a // 2, a % 2
    right = 2 * low + (1 - high)
    left = 2 * (1 - low) + high

    places = {"a": a, "right": right, "left": left, "far": 3 - a}
    ids = {
        (dz, name): (z + dz) * INNER + place
        for dz in range(1 - line, line)
        for name, place in places.items()
    }
    exists = {dz: (z + dz >= 0) & (z + dz < line) for dz in range(1 - line, line)}
    def slot(m, src, t):
        first = pl.multiple_of((src * 2 + t) * chunk, chunk)
        return gathered.at[m, :, pl.ds(first, chunk), :]

    def own_copy(m, t):
        first = pl.multiple_of((mine * 2 + t) * chunk, chunk)
        return [
            pltpu.make_async_copy(
                checkpoints_hbm.at[m, t, :, c],
                gathered.at[m, i, pl.ds(first, chunk), :],
                own_sem.at[(m * 2 + t) * len(cols) + i],
            )
            for i, c in enumerate(cols)
        ]

    for m in range(members):
        for t in range(2):
            for copy in own_copy(m, t):
                copy.start()

    count = len(cols)
    load_probes = [
        pltpu.make_async_copy(probes_hbm.at[:, :, c], probes_in.at[:, i], load_sem.at[i])
        for i, c in enumerate(cols)
    ]
    load_coefficient = [
        pltpu.make_async_copy(coefficient_hbm.at[:, c], coefficient_in.at[i], load_sem.at[count + i])
        for i, c in enumerate(cols)
    ]
    load_receiver = [
        pltpu.make_async_copy(receiver_hbm.at[:, c], receiver_in.at[i], load_sem.at[2 * count + i])
        for i, c in enumerate(cols)
    ]
    load_coarse = [pltpu.make_async_copy(coarse_hbm, coarse_in, load_sem.at[3 * count])]
    for load in load_coefficient + load_receiver + load_probes + load_coarse:
        load.start()

    barrier = pltpu.get_barrier_semaphore()

    def greet(device):
        pl.semaphore_signal(barrier, inc=1, device_id=device, device_id_type=MESH)

    greet({"probe": ids[0, "right"]})
    greet({"probe": ids[0, "left"]})

    for dz in range(1 - line, line):
        if dz:

            @pl.when(exists[dz])
            def _(dz=dz):
                greet({"probe": ids[dz, "a"]})

    for away in range(1, num_shot_devices):
        greet({"shot": (shot + away) % num_shot_devices})
    pl.semaphore_wait(barrier, line - 1 + 2 + num_shot_devices - 1)

    sent = []

    def send(m, src, t, target, sem, cond=None):
        def copy():
            return pltpu.make_async_remote_copy(
                src_ref=slot(m, ids[src], t),
                dst_ref=slot(m, ids[src], t),
                send_sem=sem(),
                recv_sem=recv_sem.at[m * flags + ids[src] * 2 + t],
                device_id={"probe": ids[target]},
                device_id_type=MESH,
            )

        copy().start()
        sent.append((copy, cond))

    def arrive(m, src, t):
        pltpu.make_async_remote_copy(
            src_ref=slot(m, ids[src], t),
            dst_ref=slot(m, ids[src], t),
            send_sem=send_sem.at[m * flags + ids[src] * 2 + t],
            recv_sem=recv_sem.at[m * flags + ids[src] * 2 + t],
            device_id={"probe": ids[0, "right"]},
            device_id_type=MESH,
        ).wait_recv()

    def ring(m, src, t, name, cond=None):
        lane = 0 if name == "right" else 1
        send(
            m,
            src,
            t,
            (0, name),
            lambda: send_sem.at[(lane * members + m) * flags + ids[src] * 2 + t],
            cond,
        )

    def spread(m, src, cond=None):
        for t in (0, 1):
            ring(m, src, t, "right", cond)
            ring(m, src, 1 - t, "left", cond)

    def begin(m):
        for t in range(2):
            for copy in own_copy(m, t):
                copy.wait()
        for k in range(1, line):
            for dz in (k, -k):

                @pl.when(exists[dz])
                def _(dz=dz):
                    for t in (0, 1):
                        index = ((dz + line - 1) * members + m) * 2 + t
                        send(m, (0, "a"), t, (dz, "a"), lambda index=index: line_sem.at[index], exists[dz])

        spread(m, (0, "a"))

    def column(m, k):
        for dz, here in sides(k):

            @pl.when(here)
            def _(dz=dz, here=here):
                for t in (0, 1):
                    arrive(m, (dz, "a"), t)
                spread(m, (dz, "a"), here)

    def sides(k):
        if k == 0:
            return ((0, None),)
        return ((-k, exists[-k]), (k, exists[k]))

    def guarded(cond, fun):
        if cond is None:
            fun()
        else:
            pl.when(cond)(fun)

    def relay(m, k):
        for dz, cond in sides(k):

            def run(dz=dz, cond=cond):
                arrive(m, (dz, "left"), 0)
                ring(m, (dz, "left"), 0, "right", cond)
                arrive(m, (dz, "right"), 1)
                ring(m, (dz, "right"), 1, "left", cond)

            guarded(cond, run)

    def finish(m, k):
        for dz, cond in sides(k):

            def run(dz=dz):
                arrive(m, (dz, "left"), 1)
                arrive(m, (dz, "right"), 0)
                arrive(m, (dz, "far"), 0)
                arrive(m, (dz, "far"), 1)

            guarded(cond, run)

    def gather_steps(m):
        plan = []
        for k in range(1, line):
            plan.append(lambda k=k: column(m, k))
            plan.append(lambda k=k: relay(m, k - 1))
        plan.append(lambda: relay(m, line - 1))
        return plan

    def gather_end(m):
        for k in range(line):
            finish(m, k)

    for m in range(members):
        begin(m)

    row_in_tile = lax.broadcasted_iota(jnp.int32, (SUB, LANE), 0)
    lane_index = lax.broadcasted_iota(jnp.int32, (SUB, LANE), 1)
    at_first = lane_index == 0
    at_last = lane_index == LANE - 1

    def parity_of(rows):
        count = jnp.zeros((SUB, LANE), jnp.int32)
        for b in range(1, bounds_ref.shape[0] - 1):
            count = count + jnp.where(rows >= bounds_ref[b], 1, 0)
        return count % 2

    def prepare_sources():
        shots = wavelet_ref.shape[1]
        spacing = width // shots
        k = lax.broadcasted_iota(jnp.int32, (shots, width), 0)
        position = k * width // shots + spacing // 2
        column_index = lax.broadcasted_iota(jnp.int32, (shots, width), 1)
        onehot = jnp.where(position == column_index, 1.0, 0.0)
        for m in range(members):
            amplitude = encodings_ref[m : m + 1, :].astype(jnp.float32) * wavelet_ref[...]
            source[m, 0:steps, :] = jnp.dot(
                amplitude,
                onehot,
                precision=lax.Precision.HIGHEST,
                preferred_element_type=jnp.float32,
            )

    def strided(j):
        return pl.ds(j, SUB, stride=tiles)

    def prepare_fields(first, last):
        def body(j, carry):
            parity = parity_of(row_in_tile * tiles + j)
            for i, c in enumerate(cols):
                value = coefficient_in[i, strided(j), :]
                seen = receiver_in[i, strided(j), :]
                coef[j, :, c] = value
                centre[j, :, c] = 2.0 - 4.0 * value
                weight[j, :, c] = value * (seen * seen)
                for p in range(num_probes):
                    vec[p, j, :, c] = jnp.where(
                        parity == p % 2, probes_in[p, i, strided(j), :], 0.0
                    )
            return carry

        lax.fori_loop(first, last, body, 0, unroll=2)

    def prepare_out():
        def body(i, carry):
            first = shot * out_rows + i * SUB
            parity_out[i] = parity_of(row_in_tile + first)
            for n, c in enumerate(cols):
                rows = pl.ds(pl.multiple_of(first, SUB), SUB)
                inverse[i, :, c] = 1.0 / coefficient_in[n, rows, :]
            return carry

        lax.fori_loop(0, out_rows // SUB, body, 0, unroll=2)

    def halo(field):
        for c in cols:
            above = pltpu.roll(field[tiles, :, c], 1, 0)
            field[0, :, c] = jnp.where(row_in_tile == 0, 0.0, above)
            below = pltpu.roll(field[1, :, c], SUB - 1, 0)
            field[tiles + 1, :, c] = jnp.where(row_in_tile == SUB - 1, 0.0, below)

    def around(field, j):
        here = [field[j + 1, :, c] for c in cols]
        fore = [pltpu.roll(x, 1, 1) for x in here]
        back = [pltpu.roll(x, LANE - 1, 1) for x in here]
        near = []
        for i, c in enumerate(cols):
            west = jnp.where(at_first, fore[i - 1] if i else 0.0, fore[i])
            east = jnp.where(at_last, back[i + 1] if i + 1 < len(cols) else 0.0, back[i])
            near.append((field[j, :, c] + field[j + 2, :, c]) + (west + east))
        return here, near

    def advance(field, before, j):
        here, near = around(field, j)
        moved = []
        for i, c in enumerate(cols):
            value = centre[j, :, c] * here[i] + coef[j, :, c] * near[i]
            if before is not None:
                value = value - before(j, c)
            moved.append(value)
        return moved

    def inner(field):
        return lambda j, c: field[j + 1, :, c]

    def convert(m):
        per = tiles // chunk
        for block in range(per):

            def body(r, carry, block=block):
                j = block * chunk + r
                for i, c in enumerate(cols):
                    um[j, :, c] = gathered[
                        m, i, pl.ds((block * 2) * chunk + r, SUB, stride=2 * tiles), :
                    ]
                    value = gathered[
                        m, i, pl.ds((block * 2 + 1) * chunk + r, SUB, stride=2 * tiles), :
                    ]
                    u0[j + 1, :, c] = value
                    for p in range(num_probes):
                        d1[p, j + 1, :, c] = vec[p, j, :, c] * value
                return carry

            lax.fori_loop(0, chunk, body, 0, unroll=2)
        halo(u0)
        for p in range(num_probes):
            halo(d1.at[p])

    def forward(m, t):
        field = (u0, u1, u2)[t]
        before = (lambda j, c: um[j, :, c], inner(u0), inner(u1))[t]
        result = (u1, u2, u3)[t]
        delta = (d1, d2, d3)[t]
        delta_before = (None, d1, d2)[t]
        delta_next = (d2, d3, e4)[t]

        def body(j, first):
            moved = advance(field, before, j)
            if first:
                for i, c in enumerate(cols):
                    row = jnp.broadcast_to(source[m, t : t + 1, c], (SUB, LANE))
                    moved[i] = moved[i] + jnp.where(row_in_tile == SUB // 2, row, 0.0)
            for i, c in enumerate(cols):
                result[j + 1, :, c] = moved[i]
            for p in range(num_probes):
                prior = None if delta_before is None else inner(delta_before.at[p])
                step = advance(delta.at[p], prior, j)
                for i, c in enumerate(cols):
                    value = step[i] + vec[p, j, :, c] * moved[i]
                    if t < 2:
                        delta_next[p, j + 1, :, c] = value
                    else:
                        value = weight[j, :, c] * value
                        delta_next[p, j + 1, :, c] = value
                        gain = moved[i] * value
                        if m:
                            gain = total[p, j, :, c] + gain
                        total[p, j, :, c] = gain

        body(0, True)

        def rest(j, carry):
            body(j, False)
            return carry

        lax.fori_loop(1, tiles, rest, 0, unroll=4)
        if t < 2:
            halo(result)
        for p in range(num_probes):
            halo(delta_next.at[p])

    def adjoint(m, t, which):
        field = (e4, e3, e2)[t]
        before = (None, e4, e3)[t]
        result = (e3, e2, None)[t]
        delta = (d3, d2, d1)[t]
        level = (u2, u1, u0)[t]

        def body(j, carry):
            for p in which:
                prior = None if before is None else inner(before.at[p])
                step = advance(field.at[p], prior, j)
                for i, c in enumerate(cols):
                    value = step[i] + weight[j, :, c] * delta[p, j + 1, :, c]
                    if result is not None:
                        result[p, j + 1, :, c] = value
                    gain = total[p, j, :, c] + level[j + 1, :, c] * value
                    if result is None and m == members - 1:
                        flat[p, i, strided(j), :] = gain
                    else:
                        total[p, j, :, c] = gain
            return carry

        lax.fori_loop(0, tiles, body, 0, unroll=4)
        if result is not None:
            for p in which:
                halo(result.at[p])

    def swap(p):
        copies = []
        for away in range(1, num_shot_devices):
            other = (shot + away) % num_shot_devices
            copies.append(
                pltpu.make_async_remote_copy(
                    src_ref=flat.at[p, :, pl.ds(pl.multiple_of(other * out_rows, SUB), out_rows), :],
                    dst_ref=partial.at[away - 1, p],
                    send_sem=swap_send.at[away - 1, p],
                    recv_sem=swap_recv.at[away - 1, p],
                    device_id={"shot": other},
                    device_id_type=MESH,
                )
            )
        return copies

    def combine(p):
        def body(i, carry):
            first = pl.multiple_of(shot * out_rows + i * SUB, SUB)
            local = pl.ds(pl.multiple_of(i * SUB, SUB), SUB)
            keep = parity_out[i] != p % 2
            for n, c in enumerate(cols):
                value = flat[p, n, pl.ds(first, SUB), :]
                for away in range(1, num_shot_devices):
                    value = value + partial[away - 1, p, n, local, :]
                value = value * inverse[i, :, c] - coarse_in[p, local, c]
                out_ref[p, local, c] = jnp.where(keep, value, 0.0)
            return carry

        lax.fori_loop(0, out_rows // SUB, body, 0)

    everything = tuple(range(num_probes))
    prepare_sources()
    for load in load_coefficient + load_receiver + load_probes:
        load.wait()
    work = []
    for q in range(4):
        work.append(lambda q=q: prepare_fields(q * tiles // 4, (q + 1) * tiles // 4))
    work.append(prepare_out)
    for step in gather_steps(0):
        step()
        if work:
            work.pop(0)()
    for rest in work:
        rest()
    load_coarse[0].wait()
    copies = [None] * num_probes
    for m in range(members):
        plan = gather_steps(m + 1) if m + 1 < members else []
        if plan:
            plan.pop(0)()
            plan.pop(0)()
        gather_end(m)
        stages = [lambda: convert(m)]
        stages += [lambda t=t: forward(m, t) for t in range(3)]
        stages += [lambda t=t: adjoint(m, t, everything) for t in range(2)]
        if m < members - 1:
            stages.append(lambda: adjoint(m, 2, everything))
        for stage in stages:
            stage()
            if plan:
                plan.pop(0)()
        for step in plan:
            step()
    for p in everything:
        adjoint(members - 1, 2, (p,))
        copies[p] = swap(p)
        for copy in copies[p]:
            copy.start()
    for p in everything:
        for copy in copies[p]:
            copy.wait_recv()
        combine(p)
    for p in everything:
        for copy in copies[p]:
            copy.wait_send()
    for copy, cond in sent:
        guarded(cond, lambda copy=copy: copy().wait_send())


def on_device(
    num_shot_devices,
    num_probe_devices,
    probes,
    coarse_sample,
    coefficient,
    receiver,
    checkpoints,
    encodings,
    wavelet,
    bounds,
):
    members, levels, chunk, width = checkpoints.shape
    num_probes, num_rows, _ = probes.shape
    out_rows = coarse_sample.shape[1]
    tiles = num_rows // SUB
    groups = width // LANE
    line = num_probe_devices // INNER
    f32 = jnp.float32

    def plain(*lead):
        return pltpu.VMEM((*lead, tiles, SUB, width), f32)

    def ringed(*lead):
        return pltpu.VMEM((*lead, tiles + 2, SUB, width), f32)

    others = num_shot_devices - 1
    anywhere = pl.BlockSpec(memory_space=pl.ANY)
    vmem = pl.BlockSpec(memory_space=pltpu.VMEM)
    return pl.pallas_call(
        functools.partial(kernel, num_shot_devices, num_probe_devices),
        out_shape=jax.ShapeDtypeStruct(coarse_sample.shape, f32),
        in_specs=[pl.BlockSpec(memory_space=pltpu.SMEM), vmem, vmem] + [anywhere] * 5,
        out_specs=vmem,
        scratch_shapes=[
            pltpu.VMEM((members, groups, levels * num_rows, LANE), f32),
            pltpu.VMEM((num_probes, groups, num_rows, LANE), f32),
            pltpu.VMEM(coarse_sample.shape, f32),
            pltpu.VMEM((groups, num_rows, LANE), f32),
            pltpu.VMEM((groups, num_rows, LANE), f32),
            plain(),
            plain(),
            plain(),
            plain(num_probes),
            plain(),
            ringed(),
            ringed(),
            ringed(),
            ringed(),
            ringed(num_probes),
            ringed(num_probes),
            ringed(num_probes),
            ringed(num_probes),
            ringed(num_probes),
            ringed(num_probes),
            plain(num_probes),
            pltpu.VMEM((num_probes, groups, num_rows, LANE), f32),
            pltpu.VMEM((others, num_probes, groups, out_rows, LANE), f32),
            pltpu.VMEM((out_rows // SUB, SUB, width), f32),
            pltpu.VMEM((out_rows // SUB, SUB, LANE), jnp.int32),
            pltpu.VMEM((members, SUB, width), f32),
            pltpu.SemaphoreType.DMA((3 * groups + 1,)),
            pltpu.SemaphoreType.DMA((members * levels * groups,)),
            pltpu.SemaphoreType.DMA((members * num_probe_devices * levels,)),
            pltpu.SemaphoreType.DMA((2 * members * num_probe_devices * levels,)),
            pltpu.SemaphoreType.DMA(((2 * line - 1) * members * levels,)),
            pltpu.SemaphoreType.DMA((others, num_probes)),
            pltpu.SemaphoreType.DMA((others, num_probes)),
        ],
        compiler_params=pltpu.CompilerParams(
            collective_id=0, has_side_effects=True, vmem_limit_bytes=60 * 1024 * 1024
        ),
    )(
        bounds,
        encodings,
        wavelet,
        probes,
        coarse_sample,
        coefficient,
        receiver,
        checkpoints,
    )


def solution(mesh):
    return jax.shard_map(
        functools.partial(on_device, mesh.shape["shot"], mesh.shape["probe"]),
        mesh=mesh,
        in_specs=(
            P("probe", None, None),
            P("probe", "shot", None),
            P(),
            P(),
            P("shot", None, "probe", None),
            P("shot", None),
            P(),
            P(),
        ),
        out_specs=P("probe", "shot", None),
        check_vma=False,
    )
```

```python
import functools

import jax
import jax.numpy as jnp
from jax import lax
from jax.experimental import pallas as pl
from jax.experimental.pallas import tpu as pltpu
from jax.sharding import PartitionSpec as P

MESH = pl.DeviceIdType.MESH
SUB = 8
LANE = 128
INNER = 4


def kernel(
    num_shot_devices,
    num_probe_devices,
    bounds_ref,
    encodings_ref,
    wavelet_ref,
    probes_hbm,
    coarse_hbm,
    coefficient_hbm,
    receiver_hbm,
    checkpoints_hbm,
    out_ref,
    gathered,
    probes_in,
    coarse_in,
    coefficient_in,
    receiver_in,
    coef,
    centre,
    weight,
    vec,
    um,
    u0,
    u1,
    u2,
    u3,
    d1,
    d2,
    d3,
    e4,
    e3,
    e2,
    total,
    flat,
    partial,
    inverse,
    parity_out,
    source,
    load_sem,
    own_sem,
    recv_sem,
    send_sem,
    line_sem,
    swap_send,
    swap_recv,
):
    members, _, chunk, width = checkpoints_hbm.shape
    num_probes, num_rows, _ = probes_hbm.shape
    out_rows = coarse_hbm.shape[1]
    tiles = num_rows // SUB
    cols = [pl.ds(c * LANE, LANE) for c in range(width // LANE)]
    steps = wavelet_ref.shape[0]
    line = num_probe_devices // INNER
    flags = num_probe_devices * 2

    shot = lax.axis_index("shot")
    mine = lax.axis_index("probe")
    z = mine // INNER
    a = mine % INNER
    high, low = a // 2, a % 2
    right = 2 * low + (1 - high)
    left = 2 * (1 - low) + high

    places = {"a": a, "right": right, "left": left, "far": 3 - a}
    ids = {
        (dz, name): (z + dz) * INNER + place
        for dz in range(1 - line, line)
        for name, place in places.items()
    }
    exists = {dz: (z + dz >= 0) & (z + dz < line) for dz in range(1 - line, line)}
    def slot(m, src, t):
        first = pl.multiple_of((src * 2 + t) * chunk, chunk)
        return gathered.at[m, :, pl.ds(first, chunk), :]

    def own_copy(m, t):
        first = pl.multiple_of((mine * 2 + t) * chunk, chunk)
        return [
            pltpu.make_async_copy(
                checkpoints_hbm.at[m, t, :, c],
                gathered.at[m, i, pl.ds(first, chunk), :],
                own_sem.at[(m * 2 + t) * len(cols) + i],
            )
            for i, c in enumerate(cols)
        ]

    for m in range(members):
        for t in range(2):
            for copy in own_copy(m, t):
                copy.start()

    count = len(cols)
    load_probes = [
        pltpu.make_async_copy(probes_hbm.at[:, :, c], probes_in.at[:, i], load_sem.at[i])
        for i, c in enumerate(cols)
    ]
    load_coefficient = [
        pltpu.make_async_copy(coefficient_hbm.at[:, c], coefficient_in.at[i], load_sem.at[count + i])
        for i, c in enumerate(cols)
    ]
    load_receiver = [
        pltpu.make_async_copy(receiver_hbm.at[:, c], receiver_in.at[i], load_sem.at[2 * count + i])
        for i, c in enumerate(cols)
    ]
    load_coarse = [pltpu.make_async_copy(coarse_hbm, coarse_in, load_sem.at[3 * count])]
    for load in load_coefficient + load_receiver + load_probes + load_coarse:
        load.start()

    barrier = pltpu.get_barrier_semaphore()

    def greet(device):
        pl.semaphore_signal(barrier, inc=1, device_id=device, device_id_type=MESH)

    greet({"probe": ids[0, "right"]})
    greet({"probe": ids[0, "left"]})

    for dz in range(1 - line, line):
        if dz:

            @pl.when(exists[dz])
            def _(dz=dz):
                greet({"probe": ids[dz, "a"]})

    for away in range(1, num_shot_devices):
        greet({"shot": (shot + away) % num_shot_devices})
    pl.semaphore_wait(barrier, line - 1 + 2 + num_shot_devices - 1)

    sent = []

    def send(m, src, t, target, sem, cond=None):
        def copy():
            return pltpu.make_async_remote_copy(
                src_ref=slot(m, ids[src], t),
                dst_ref=slot(m, ids[src], t),
                send_sem=sem(),
                recv_sem=recv_sem.at[m * flags + ids[src] * 2 + t],
                device_id={"probe": ids[target]},
                device_id_type=MESH,
            )

        copy().start()
        sent.append((copy, cond))

    def arrive(m, src, t):
        pltpu.make_async_remote_copy(
            src_ref=slot(m, ids[src], t),
            dst_ref=slot(m, ids[src], t),
            send_sem=send_sem.at[m * flags + ids[src] * 2 + t],
            recv_sem=recv_sem.at[m * flags + ids[src] * 2 + t],
            device_id={"probe": ids[0, "right"]},
            device_id_type=MESH,
        ).wait_recv()

    def ring(m, src, t, name, cond=None):
        lane = 0 if name == "right" else 1
        send(
            m,
            src,
            t,
            (0, name),
            lambda: send_sem.at[(lane * members + m) * flags + ids[src] * 2 + t],
            cond,
        )

    def spread(m, src, cond=None):
        for t in (0, 1):
            ring(m, src, t, "right", cond)
            ring(m, src, 1 - t, "left", cond)

    def begin(m):
        for t in range(2):
            for copy in own_copy(m, t):
                copy.wait()
        for k in range(1, line):
            for dz in (k, -k):

                @pl.when(exists[dz])
                def _(dz=dz):
                    for t in (0, 1):
                        index = ((dz + line - 1) * members + m) * 2 + t
                        send(m, (0, "a"), t, (dz, "a"), lambda index=index: line_sem.at[index], exists[dz])

        spread(m, (0, "a"))

    def column(m, k):
        for dz, here in sides(k):

            @pl.when(here)
            def _(dz=dz, here=here):
                for t in (0, 1):
                    arrive(m, (dz, "a"), t)
                spread(m, (dz, "a"), here)

    def sides(k):
        if k == 0:
            return ((0, None),)
        return ((-k, exists[-k]), (k, exists[k]))

    def guarded(cond, fun):
        if cond is None:
            fun()
        else:
            pl.when(cond)(fun)

    def relay(m, k):
        for dz, cond in sides(k):

            def run(dz=dz, cond=cond):
                arrive(m, (dz, "left"), 0)
                ring(m, (dz, "left"), 0, "right", cond)
                arrive(m, (dz, "right"), 1)
                ring(m, (dz, "right"), 1, "left", cond)

            guarded(cond, run)

    def finish(m, k):
        for dz, cond in sides(k):

            def run(dz=dz):
                arrive(m, (dz, "left"), 1)
                arrive(m, (dz, "right"), 0)
                arrive(m, (dz, "far"), 0)
                arrive(m, (dz, "far"), 1)

            guarded(cond, run)

    def gather_steps(m):
        plan = []
        for k in range(1, line):
            plan.append(lambda k=k: column(m, k))
        for k in range(line):
            plan.append(lambda k=k: relay(m, k))
        return plan

    def gather_end(m):
        for k in range(line):
            finish(m, k)

    for m in range(members):
        begin(m)

    row_in_tile = lax.broadcasted_iota(jnp.int32, (SUB, LANE), 0)
    lane_index = lax.broadcasted_iota(jnp.int32, (SUB, LANE), 1)
    at_first = lane_index == 0
    at_last = lane_index == LANE - 1

    def parity_of(rows):
        count = jnp.zeros((SUB, LANE), jnp.int32)
        for b in range(1, bounds_ref.shape[0] - 1):
            count = count + jnp.where(rows >= bounds_ref[b], 1, 0)
        return count % 2

    def prepare_sources():
        shots = wavelet_ref.shape[1]
        spacing = width // shots
        k = lax.broadcasted_iota(jnp.int32, (shots, width), 0)
        position = k * width // shots + spacing // 2
        column_index = lax.broadcasted_iota(jnp.int32, (shots, width), 1)
        onehot = jnp.where(position == column_index, 1.0, 0.0)
        for m in range(members):
            amplitude = encodings_ref[m : m + 1, :].astype(jnp.float32) * wavelet_ref[...]
            source[m, 0:steps, :] = jnp.dot(
                amplitude,
                onehot,
                precision=lax.Precision.HIGHEST,
                preferred_element_type=jnp.float32,
            )

    def strided(j):
        return pl.ds(j, SUB, stride=tiles)

    def prepare_fields(first, last):
        def body(j, carry):
            parity = parity_of(row_in_tile * tiles + j)
            for i, c in enumerate(cols):
                value = coefficient_in[i, strided(j), :]
                seen = receiver_in[i, strided(j), :]
                coef[j, :, c] = value
                centre[j, :, c] = 2.0 - 4.0 * value
                weight[j, :, c] = value * (seen * seen)
                for p in range(num_probes):
                    vec[p, j, :, c] = jnp.where(
                        parity == p % 2, probes_in[p, i, strided(j), :], 0.0
                    )
            return carry

        lax.fori_loop(first, last, body, 0, unroll=2)

    def prepare_out():
        def body(i, carry):
            first = shot * out_rows + i * SUB
            parity_out[i] = parity_of(row_in_tile + first)
            for n, c in enumerate(cols):
                rows = pl.ds(pl.multiple_of(first, SUB), SUB)
                inverse[i, :, c] = 1.0 / coefficient_in[n, rows, :]
            return carry

        lax.fori_loop(0, out_rows // SUB, body, 0, unroll=2)

    def halo(field):
        for c in cols:
            above = pltpu.roll(field[tiles, :, c], 1, 0)
            field[0, :, c] = jnp.where(row_in_tile == 0, 0.0, above)
            below = pltpu.roll(field[1, :, c], SUB - 1, 0)
            field[tiles + 1, :, c] = jnp.where(row_in_tile == SUB - 1, 0.0, below)

    def around(field, j):
        here = [field[j + 1, :, c] for c in cols]
        fore = [pltpu.roll(x, 1, 1) for x in here]
        back = [pltpu.roll(x, LANE - 1, 1) for x in here]
        near = []
        for i, c in enumerate(cols):
            west = jnp.where(at_first, fore[i - 1] if i else 0.0, fore[i])
            east = jnp.where(at_last, back[i + 1] if i + 1 < len(cols) else 0.0, back[i])
            near.append((field[j, :, c] + field[j + 2, :, c]) + (west + east))
        return here, near

    def advance(field, before, j):
        here, near = around(field, j)
        moved = []
        for i, c in enumerate(cols):
            value = centre[j, :, c] * here[i] + coef[j, :, c] * near[i]
            if before is not None:
                value = value - before(j, c)
            moved.append(value)
        return moved

    def inner(field):
        return lambda j, c: field[j + 1, :, c]

    def convert(m):
        per = tiles // chunk
        for block in range(per):

            def body(r, carry, block=block):
                j = block * chunk + r
                for i, c in enumerate(cols):
                    um[j, :, c] = gathered[
                        m, i, pl.ds((block * 2) * chunk + r, SUB, stride=2 * tiles), :
                    ]
                    value = gathered[
                        m, i, pl.ds((block * 2 + 1) * chunk + r, SUB, stride=2 * tiles), :
                    ]
                    u0[j + 1, :, c] = value
                    for p in range(num_probes):
                        d1[p, j + 1, :, c] = vec[p, j, :, c] * value
                return carry

            lax.fori_loop(0, chunk, body, 0, unroll=2)
        halo(u0)
        for p in range(num_probes):
            halo(d1.at[p])

    def forward(m, t):
        field = (u0, u1, u2)[t]
        before = (lambda j, c: um[j, :, c], inner(u0), inner(u1))[t]
        result = (u1, u2, u3)[t]
        delta = (d1, d2, d3)[t]
        delta_before = (None, d1, d2)[t]
        delta_next = (d2, d3, e4)[t]

        def body(j, first):
            moved = advance(field, before, j)
            if first:
                for i, c in enumerate(cols):
                    row = jnp.broadcast_to(source[m, t : t + 1, c], (SUB, LANE))
                    moved[i] = moved[i] + jnp.where(row_in_tile == SUB // 2, row, 0.0)
            for i, c in enumerate(cols):
                result[j + 1, :, c] = moved[i]
            for p in range(num_probes):
                prior = None if delta_before is None else inner(delta_before.at[p])
                step = advance(delta.at[p], prior, j)
                for i, c in enumerate(cols):
                    value = step[i] + vec[p, j, :, c] * moved[i]
                    if t < 2:
                        delta_next[p, j + 1, :, c] = value
                    else:
                        value = weight[j, :, c] * value
                        delta_next[p, j + 1, :, c] = value
                        gain = moved[i] * value
                        if m:
                            gain = total[p, j, :, c] + gain
                        total[p, j, :, c] = gain

        body(0, True)

        def rest(j, carry):
            body(j, False)
            return carry

        lax.fori_loop(1, tiles, rest, 0, unroll=4)
        if t < 2:
            halo(result)
        for p in range(num_probes):
            halo(delta_next.at[p])

    def adjoint(m, t, which):
        field = (e4, e3, e2)[t]
        before = (None, e4, e3)[t]
        result = (e3, e2, None)[t]
        delta = (d3, d2, d1)[t]
        level = (u2, u1, u0)[t]

        def body(j, carry):
            for p in which:
                prior = None if before is None else inner(before.at[p])
                step = advance(field.at[p], prior, j)
                for i, c in enumerate(cols):
                    value = step[i] + weight[j, :, c] * delta[p, j + 1, :, c]
                    if result is not None:
                        result[p, j + 1, :, c] = value
                    gain = total[p, j, :, c] + level[j + 1, :, c] * value
                    if result is None and m == members - 1:
                        flat[p, i, strided(j), :] = gain
                    else:
                        total[p, j, :, c] = gain
            return carry

        lax.fori_loop(0, tiles, body, 0, unroll=4)
        if result is not None:
            for p in which:
                halo(result.at[p])

    def swap(p):
        copies = []
        for away in range(1, num_shot_devices):
            other = (shot + away) % num_shot_devices
            copies.append(
                pltpu.make_async_remote_copy(
                    src_ref=flat.at[p, :, pl.ds(pl.multiple_of(other * out_rows, SUB), out_rows), :],
                    dst_ref=partial.at[away - 1, p],
                    send_sem=swap_send.at[away - 1, p],
                    recv_sem=swap_recv.at[away - 1, p],
                    device_id={"shot": other},
                    device_id_type=MESH,
                )
            )
        return copies

    def combine(p):
        def body(i, carry):
            first = pl.multiple_of(shot * out_rows + i * SUB, SUB)
            local = pl.ds(pl.multiple_of(i * SUB, SUB), SUB)
            keep = parity_out[i] != p % 2
            for n, c in enumerate(cols):
                value = flat[p, n, pl.ds(first, SUB), :]
                for away in range(1, num_shot_devices):
                    value = value + partial[away - 1, p, n, local, :]
                value = value * inverse[i, :, c] - coarse_in[p, local, c]
                out_ref[p, local, c] = jnp.where(keep, value, 0.0)
            return carry

        lax.fori_loop(0, out_rows // SUB, body, 0)

    everything = tuple(range(num_probes))
    prepare_sources()
    for load in load_coefficient + load_receiver + load_probes:
        load.wait()
    work = []
    for q in range(4):
        work.append(lambda q=q: prepare_fields(q * tiles // 4, (q + 1) * tiles // 4))
    work.append(prepare_out)
    for step in gather_steps(0):
        step()
        if work:
            work.pop(0)()
    for rest in work:
        rest()
    load_coarse[0].wait()
    copies = [None] * num_probes
    for m in range(members):
        plan = gather_steps(m + 1) if m + 1 < members else []
        if plan:
            for _ in range(line - 1):
                plan.pop(0)()
        gather_end(m)
        stages = [lambda: convert(m)]
        stages += [lambda t=t: forward(m, t) for t in range(3)]
        stages += [lambda t=t: adjoint(m, t, everything) for t in range(2)]
        if m < members - 1:
            stages.append(lambda: adjoint(m, 2, everything))
        for stage in stages:
            stage()
            if plan:
                plan.pop(0)()
        for step in plan:
            step()
    for p in everything:
        adjoint(members - 1, 2, (p,))
        copies[p] = swap(p)
        for copy in copies[p]:
            copy.start()
    for p in everything:
        for copy in copies[p]:
            copy.wait_recv()
        combine(p)
    for p in everything:
        for copy in copies[p]:
            copy.wait_send()
    for copy, cond in sent:
        guarded(cond, lambda copy=copy: copy().wait_send())


def on_device(
    num_shot_devices,
    num_probe_devices,
    probes,
    coarse_sample,
    coefficient,
    receiver,
    checkpoints,
    encodings,
    wavelet,
    bounds,
):
    members, levels, chunk, width = checkpoints.shape
    num_probes, num_rows, _ = probes.shape
    out_rows = coarse_sample.shape[1]
    tiles = num_rows // SUB
    groups = width // LANE
    line = num_probe_devices // INNER
    f32 = jnp.float32

    def plain(*lead):
        return pltpu.VMEM((*lead, tiles, SUB, width), f32)

    def ringed(*lead):
        return pltpu.VMEM((*lead, tiles + 2, SUB, width), f32)

    others = num_shot_devices - 1
    anywhere = pl.BlockSpec(memory_space=pl.ANY)
    vmem = pl.BlockSpec(memory_space=pltpu.VMEM)
    return pl.pallas_call(
        functools.partial(kernel, num_shot_devices, num_probe_devices),
        out_shape=jax.ShapeDtypeStruct(coarse_sample.shape, f32),
        in_specs=[pl.BlockSpec(memory_space=pltpu.SMEM), vmem, vmem] + [anywhere] * 5,
        out_specs=vmem,
        scratch_shapes=[
            pltpu.VMEM((members, groups, levels * num_rows, LANE), f32),
            pltpu.VMEM((num_probes, groups, num_rows, LANE), f32),
            pltpu.VMEM(coarse_sample.shape, f32),
            pltpu.VMEM((groups, num_rows, LANE), f32),
            pltpu.VMEM((groups, num_rows, LANE), f32),
            plain(),
            plain(),
            plain(),
            plain(num_probes),
            plain(),
            ringed(),
            ringed(),
            ringed(),
            ringed(),
            ringed(num_probes),
            ringed(num_probes),
            ringed(num_probes),
            ringed(num_probes),
            ringed(num_probes),
            ringed(num_probes),
            plain(num_probes),
            pltpu.VMEM((num_probes, groups, num_rows, LANE), f32),
            pltpu.VMEM((others, num_probes, groups, out_rows, LANE), f32),
            pltpu.VMEM((out_rows // SUB, SUB, width), f32),
            pltpu.VMEM((out_rows // SUB, SUB, LANE), jnp.int32),
            pltpu.VMEM((members, SUB, width), f32),
            pltpu.SemaphoreType.DMA((3 * groups + 1,)),
            pltpu.SemaphoreType.DMA((members * levels * groups,)),
            pltpu.SemaphoreType.DMA((members * num_probe_devices * levels,)),
            pltpu.SemaphoreType.DMA((2 * members * num_probe_devices * levels,)),
            pltpu.SemaphoreType.DMA(((2 * line - 1) * members * levels,)),
            pltpu.SemaphoreType.DMA((others, num_probes)),
            pltpu.SemaphoreType.DMA((others, num_probes)),
        ],
        compiler_params=pltpu.CompilerParams(
            collective_id=0, has_side_effects=True, vmem_limit_bytes=60 * 1024 * 1024
        ),
    )(
        bounds,
        encodings,
        wavelet,
        probes,
        coarse_sample,
        coefficient,
        receiver,
        checkpoints,
    )


def solution(mesh):
    return jax.shard_map(
        functools.partial(on_device, mesh.shape["shot"], mesh.shape["probe"]),
        mesh=mesh,
        in_specs=(
            P("probe", None, None),
            P("probe", "shot", None),
            P(),
            P(),
            P("shot", None, "probe", None),
            P("shot", None),
            P(),
            P(),
        ),
        out_specs=P("probe", "shot", None),
        check_vma=False,
    )
```
